256 devices in a mesh: gx: 32 (over x_hi, z, core), gy: 8 (over x_lo, y).
Axes of the slice: x: 4 (x_hi: 2, x_lo: 2; x = x_hi * 2 + x_lo), y: 4, z: 8, core: 2. Of those that a mesh axis runs over, the one named last changes fastest.
Arguments:
- chemical_share_array: float32 [16, 8, 1024, 2048], P(None, None, 'gx', 'gy'), may hold values from 0 to 1
- horizontal_motion: float32 [8, 1024, 2048], P(None, 'gx', 'gy'), may hold values from -8 to 8
- vertical_motion: float32 [8, 1024, 2048], P(None, 'gx', 'gy'), may hold values from -8 to 8
- nondimensional_thermal_value: float32 [8, 1024, 2048], P(None, 'gx', 'gy'), may hold values from 0.8 to 2
- collision_prefactors_array: float32 [32], replicated, may hold values from 0.3 to 3
- activation_thresholds: float32 [32], replicated, may hold values from 0.5 to 4
- stoichiometry_table: float32 [32, 16], replicated, may hold values from -4 to 4
- transverse_loading_horizontal: float32 [1024, 64], P('gx'), may hold values from -0.1875 to 0.1875
- transverse_loading_vertical: float32 [2048, 64], P('gy'), may hold values from -0.125 to 0.125
Outputs:
- new_state: float32 [16, 8, 1024, 2048], P(None, None, 'gx', 'gy')
- core_part: float32 [64, 64, 128], P('gx', 'gy')
The draws below stay inside these ranges and needn't reach their ends.
All inputs are finite; a program needn't handle non-finite values.
Results may differ from the reference program's by a relative error of at most 0.000094.
Values sent between devices are 32-bit elements; how exact they have to be, the bound alone decides.
A program may use at most 128 MiB of HBM per device.

```python
import math
import jax
import jax.numpy as jnp
import numpy as np
from jax import lax

NS = 16
RATE_LAWS_TOTAL = 32
RANK = 64
LAYER_COUNT_DEEP = 8
MESH_COUNT_EAST = 1024
MESH_COUNT_NORTH = 2048


def block_levels(stream_key, shape, shards, smallest, high):
    def one(dim, parts):
        steps = jax.random.uniform(jax.random.fold_in(jax.random.fold_in(stream_key, 6), dim), (parts,), jnp.float32, smallest / len(shards), high / len(shards))
        return jnp.repeat(jnp.exp(steps), shape[dim] // parts).reshape((-1,) + (1,) * (len(shape) - dim - 1))

    level = one(*shards[0])
    for cut in shards[1:]:
        level = level * one(*cut)
    return level


def normal_values(stream_key, extent, spread, limit, split=(), dtype=jnp.bfloat16):
    array = spread * jax.random.normal(stream_key, extent, jnp.float32)
    if split:
        array = array * block_levels(stream_key, extent, split, -0.22, 0.18)
    return jnp.clip(array, -limit, limit).astype(dtype)


def setup_inputs(seed: int = 0) -> dict:
    keys = jax.random.split(jax.random.key(seed), 10)
    chemical_share_array = jnp.clip(1.0 * jax.random.uniform(keys[0], (NS, LAYER_COUNT_DEEP, MESH_COUNT_EAST, MESH_COUNT_NORTH), jnp.float32) ** block_levels(keys[0], (NS, LAYER_COUNT_DEEP, MESH_COUNT_EAST, MESH_COUNT_NORTH), ((2, 32), (3, 8)), -0.2, 0.2), 0.0, 1.0)
    horizontal_motion = normal_values(keys[1], (LAYER_COUNT_DEEP, MESH_COUNT_EAST, MESH_COUNT_NORTH), 2.0, 8.0, ((1, 32), (2, 8)), jnp.float32)
    vertical_motion = normal_values(keys[2], (LAYER_COUNT_DEEP, MESH_COUNT_EAST, MESH_COUNT_NORTH), 2.0, 8.0, ((1, 32), (2, 8)), jnp.float32)
    nondimensional_thermal_value = jnp.clip(0.8 + 1.2 * jax.random.uniform(keys[3], (LAYER_COUNT_DEEP, MESH_COUNT_EAST, MESH_COUNT_NORTH), jnp.float32) ** block_levels(keys[3], (LAYER_COUNT_DEEP, MESH_COUNT_EAST, MESH_COUNT_NORTH), ((1, 32), (2, 8)), -0.2, 0.2), 0.8, 2.0)
    collision_prefactors_array = jnp.clip(jnp.exp(jax.random.uniform(keys[4], (RATE_LAWS_TOTAL,), jnp.float32, math.log(0.3), math.log(3.0))), 0.3, 3.0)
    activation_thresholds = jnp.clip(jnp.exp(jax.random.uniform(keys[5], (RATE_LAWS_TOTAL,), jnp.float32, math.log(0.5), math.log(4.0))), 0.5, 4.0)
    stoichiometry_table = normal_values(keys[6], (RATE_LAWS_TOTAL, NS), 0.7, 4.0, (), jnp.float32)
    transverse_loading_horizontal = normal_values(keys[7], (MESH_COUNT_EAST, RANK), MESH_COUNT_EAST ** -0.5, 0.1875, ((0, 32),), jnp.float32)
    transverse_loading_vertical = normal_values(keys[8], (MESH_COUNT_NORTH, RANK), MESH_COUNT_NORTH ** -0.5, 0.125, ((0, 8),), jnp.float32)
    return {"chemical_share_array": chemical_share_array, "horizontal_motion": horizontal_motion, "vertical_motion": vertical_motion, "nondimensional_thermal_value": nondimensional_thermal_value, "collision_prefactors_array": collision_prefactors_array, "activation_thresholds": activation_thresholds, "stoichiometry_table": stoichiometry_table, "transverse_loading_horizontal": transverse_loading_horizontal, "transverse_loading_vertical": transverse_loading_vertical}


first_coef = (0.8, -0.2, 4.0 / 105.0, -1.0 / 280.0)
second_coef = (-205.0 / 72.0, 1.6, -0.2, 8.0 / 315.0, -1.0 / 560.0)
step_size = 0.5
diffusivity = 0.2


def first_deriv(field, axis):
    total = jnp.zeros_like(field)
    for offset in range(1, 5):
        total = total + first_coef[offset - 1] * (jnp.roll(field, -offset, axis) - jnp.roll(field, offset, axis))
    return total


def second_deriv(field, axis):
    total = second_coef[0] * field
    for offset in range(1, 5):
        total = total + second_coef[offset] * (jnp.roll(field, -offset, axis) + jnp.roll(field, offset, axis))
    return total


def isolated_page(argument_group, collision_prefactors_array, activation_thresholds, stoichiometry_table, transverse_loading_horizontal, transverse_loading_vertical):
    plane, vel_x, vel_y, scratch_surface = argument_group
    first_idx = np.arange(RATE_LAWS_TOTAL) % NS
    second_idx = (3 * np.arange(RATE_LAWS_TOTAL) + 1) % NS
    thermal_rate_law = collision_prefactors_array[:, None, None] * jnp.exp(-activation_thresholds[:, None, None] / scratch_surface[None])
    products = thermal_rate_law * plane[first_idx] * plane[second_idx]
    source = jnp.einsum("rs,rxy->sxy", stoichiometry_table, products, precision=lax.Precision.HIGHEST)
    rhs = -vel_x[None] * first_deriv(plane, 1) - vel_y[None] * first_deriv(plane, 2)
    rhs = rhs + diffusivity * (second_deriv(plane, 1) + second_deriv(plane, 2)) + source
    marched_result = plane + step_size * rhs
    partial_y = jnp.einsum("sxy,yj->sxj", marched_result, transverse_loading_vertical, precision=lax.Precision.HIGHEST)
    core_plane = jnp.einsum("xi,sxj->ijs", transverse_loading_horizontal, partial_y, precision=lax.Precision.HIGHEST)
    return marched_result, core_plane


def reference(chemical_share_array, horizontal_motion, vertical_motion, nondimensional_thermal_value, collision_prefactors_array, activation_thresholds, stoichiometry_table, transverse_loading_horizontal, transverse_loading_vertical):
    pile_of_pages = jnp.moveaxis(chemical_share_array, 1, 0)
    marched_result, condensed_middle_array = lax.map(lambda argument_group: isolated_page(argument_group, collision_prefactors_array, activation_thresholds, stoichiometry_table, transverse_loading_horizontal, transverse_loading_vertical), (pile_of_pages, horizontal_motion, vertical_motion, nondimensional_thermal_value))
    new_state = jnp.moveaxis(marched_result, 0, 1)
    core_part = jnp.transpose(condensed_middle_array, (1, 2, 3, 0)).reshape(RANK, RANK, NS * LAYER_COUNT_DEEP)
    return new_state, core_part
```

```python
import functools
import jax
import jax.numpy as jnp
import numpy as np
import ml_dtypes
from jax import lax
from jax.experimental import pallas as pl
from jax.experimental.pallas import tpu as pltpu
from jax.sharding import PartitionSpec as P

NS, NR, NZ = 16, 32, 8
CX, CY_ = 32, 256
RANK = 64
STEP, DIFF = 0.5, 0.2
SCALE_1, SCALE_2 = 840, 5040
D1 = (672, -168, 32, -3)
D2 = (8064, -1008, 128, -9)
CENTRE = 1.0 + STEP * DIFF * 2.0 * (-205.0 / 72.0)
K_X = -STEP / SCALE_1
K_2 = STEP * DIFF / SCALE_2
F32, BF16 = jnp.float32, jnp.bfloat16
MESH = pl.DeviceIdType.MESH
HIGHEST = lax.Precision.HIGHEST
ROWS = ((8, 16), (0, 24))
X_OF = [list(range(8, 24)), list(range(0, 8)) + list(range(24, 32))]
KEPT = X_OF[1] + X_OF[0]


def tap(kind, offset):
    if offset == 0 or abs(offset) > 4:
        return 0
    if kind == 0:
        return D1[abs(offset) - 1] * (1 if offset > 0 else -1)
    return D2[abs(offset) - 1]


def stencil_tables():
    by = np.zeros((384, 512), np.float32)
    for kind in range(2):
        for out in range(256):
            for off in range(-4, 5):
                y = out + off
                row = y if 0 <= y < 256 else (256 + (y - 256) if y >= 256 else 256 + 64 + (y + 4))
                by[row, kind * 256 + out] = tap(kind, off)
    by = np.concatenate([by[:256], by[:256], by[256:], by[256:]], axis=0)
    main = np.zeros((2, 256, 256), np.float32)
    halo = np.zeros((2, 256, 128), np.float32)
    for half in range(2):
        for kind in range(2):
            for s in range(8):
                for i, x in enumerate(X_OF[half]):
                    row = kind * 128 + s * 16 + i
                    for k, xx in enumerate(KEPT):
                        main[half, row, s * 32 + k] = tap(kind, xx - x)
    for block in range(2):
        for kind in range(2):
            for s in range(8):
                for i, x in enumerate(X_OF[1]):
                    row = kind * 128 + s * 16 + i
                    for k in range(4):
                        halo[block, row, s * 8 + block * 4 + k] = tap(kind, (k - 4) - x)
                        halo[block, row, 64 + s * 8 + block * 4 + k] = tap(kind, (32 + k) - x)
    main = np.concatenate([main, main], axis=2)
    halo = np.concatenate([halo, halo], axis=2)
    bf = ml_dtypes.bfloat16
    return by.astype(bf), main.astype(bf), halo.astype(bf)


BY, AMAIN, AHALO = stencil_tables()


def split(x):
    hi = x.astype(BF16)
    return hi, (x - hi.astype(F32)).astype(BF16)


def dot(a, b, dims=((1,), (0,)), precision=None):
    return lax.dot_general(a, b, (dims, ((), ())), precision=precision, preferred_element_type=F32)


def iota(shape, dim):
    return lax.broadcasted_iota(jnp.int32, shape, dim)


def kernel(
    remote,
    ngx,
    ngy,
    act_ref,
    pref_ref,
    stoich_ref,
    load_x_ref,
    load_y_ref,
    c_hbm,
    vx_hbm,
    vy_hbm,
    t_hbm,
    by_hbm,
    am_hbm,
    ah_hbm,
    out_ref,
    core_ref,
    c,
    vx,
    vy,
    temp,
    by,
    am,
    ah,
    cs,
    xn,
    xp,
    hp,
    hn,
    yl,
    yr,
    hl,
    hr,
    w2,
    vt2,
    xb2,
    rhi,
    rlo,
    nhi,
    nlo,
    part,
    got,
    yhi,
    ylo,
    g,
    pair_got,
    gs,
    core_got,
    load_sems,
    halo_send,
    halo_recv,
    part_send,
    part_recv,
    pair_sems,
    core_send,
    core_recv,
):
    loads = []
    for k in range(NZ):
        loads.append(pltpu.make_async_copy(c_hbm.at[:, k], c.at[:, k], load_sems.at[k]))
    for k, (src, dst) in enumerate(((vx_hbm, vx), (vy_hbm, vy), (t_hbm, temp), (by_hbm, by), (am_hbm, am), (ah_hbm, ah))):
        loads.append(pltpu.make_async_copy(src, dst, load_sems.at[NZ + k]))
    for copy in loads:
        copy.start()
    if remote:
        mx, my = lax.axis_index("gx"), lax.axis_index("gy")
        par = lax.rem(mx, 2)
        chip = mx // 2
        barrier = pltpu.get_barrier_semaphore()
        gy_peer = [lax.rem(my + d, ngy) for d in range(ngy)]
        chip_peer = [lax.rem(chip + d, ngx // 2) for d in range(ngx // 2)]
        partner = mx + 1 - 2 * par
        other = lax.rem(mx + 2 * par - 1 + ngx, ngx)
        for d in range(1, ngy):
            pl.semaphore_signal(barrier, inc=1, device_id={"gx": mx, "gy": gy_peer[d]}, device_id_type=MESH)
        for d in range(1, ngx // 2):
            pl.semaphore_signal(barrier, inc=1, device_id={"gx": 2 * chip_peer[d] + par, "gy": my}, device_id_type=MESH)
        for to in (partner, other):
            pl.semaphore_signal(barrier, inc=1, device_id={"gx": to, "gy": my}, device_id_type=MESH)

    fold = dot((iota((128, 16), 0) // 8 == iota((128, 16), 1)).astype(F32), stoich_ref[...], ((1,), (1,)), HIGHEST)
    widen = (iota((32, 256), 1) // 8 == iota((32, 256), 0)).astype(F32)
    table = dot(fold, widen, precision=HIGHEST)
    scale = dot(jnp.broadcast_to(pref_ref[...], (8, 32)), widen, precision=HIGHEST)[0:1] * STEP
    table = jnp.where(iota((128, 256), 0) % 8 == iota((128, 256), 1) % 8, table * scale, 0.0)
    hi, lo = split(table)
    w2[0:128], w2[128:256] = hi, lo
    eye = (iota((64, 64), 0) == iota((64, 64), 1)).astype(F32)
    hi, lo = split(dot(eye, load_y_ref[...], ((1,), (1,)), HIGHEST))
    vt2[0:64], vt2[64:128] = hi, lo
    row = iota((512, 64), 0) // 8
    rank = 4 * (row % 32 // 2) + 2 * (row // 32) + row % 2
    pick = (rank == iota((512, 64), 1)).astype(F32)
    col = iota((32, 256), 1)
    kept = col // 128 * 16 + col % 16
    x_of = jnp.where(kept < 16, 8 + kept, jnp.where(kept < 24, kept - 16, kept))
    spread = (x_of == iota((32, 256), 0)).astype(F32)
    wide = dot(load_x_ref[...], spread, ((0,), (0,)), HIGHEST)
    wide = dot(pick, wide, precision=HIGHEST)
    wide = jnp.where(iota((512, 256), 0) % 8 == iota((512, 256), 1) % 128 // 16, wide, 0.0)
    hi, lo = split(wide)
    xb2[0:512], xb2[512:1024] = hi, lo

    for copy in loads[:NZ]:
        copy.wait()

    def pack_y(q, carry):
        lane = iota((32, 128), 1) // 4
        left = jnp.zeros((32, 128), F32)
        right = jnp.zeros((32, 128), F32)
        for p in range(32):
            s, z = q * 4 + p // 8, p % 8
            first, last = c[s, z, :, 0:128], c[s, z, :, 128:256]
            left = jnp.where(lane == p, pltpu.roll(first, 4 * p, 1) if p else first, left)
            right = jnp.where(lane == p, pltpu.roll(last, (4 * p + 4) % 128, 1) if p < 31 else last, right)
        yl[q], yr[q] = left, right
        return carry

    lax.fori_loop(0, 4, pack_y, 0)

    def pack_x(z, carry):
        low = iota((8, 256), 0) < 4
        for s in range(8):
            xn[z, s] = jnp.where(low, pltpu.roll(c[s, z, 24:32, :], 4, 0), c[s + 8, z, 24:32, :])
            xp[z, s] = jnp.where(low, c[s, z, 0:8, :], pltpu.roll(c[s + 8, z, 0:8, :], 4, 0))
        return carry

    lax.fori_loop(0, NZ, pack_x, 0)

    if remote:
        pl.semaphore_wait(barrier, ngy - 1 + ngx // 2 - 1 + 2)
        up_x, down_x = lax.rem(mx + 1, ngx), lax.rem(mx + ngx - 1, ngx)
        targets = (
            (yr, hl, mx, gy_peer[1]),
            (yl, hr, mx, gy_peer[ngy - 1]),
            (xn, hp, up_x, my),
            (xp, hn, down_x, my),
        )
        halos = [
            pltpu.make_async_remote_copy(
                src, dst, halo_send.at[k], halo_recv.at[k], device_id={"gx": tx, "gy": ty}, device_id_type=MESH
            )
            for k, (src, dst, tx, ty) in enumerate(targets)
        ]
    else:
        halos = [
            pltpu.make_async_copy(src, dst, halo_recv.at[k])
            for k, (src, dst) in enumerate(((yr, hl), (yl, hr), (xn, hp), (xp, hn)))
        ]
    for copy in halos:
        copy.start()

    def presplit(z, carry):
        for s in range(NS):
            for k, (a, b) in enumerate((ROWS[1], ROWS[0])):
                both = jnp.concatenate([c[s, z, a : a + 8, :], c[s, z, b : b + 8, :]], axis=0)
                hi, lo = split(both)
                cs[s, z, 16 * k : 16 * k + 16, 0:256] = hi
                cs[s, z, 16 * k : 16 * k + 16, 256:512] = lo
        return carry

    lax.fori_loop(0, NZ, presplit, 0)
    for copy in loads[NZ:]:
        copy.wait()

    def landed(copy):
        if remote:
            copy.wait_recv()
        else:
            copy.wait()

    landed(halos[0])
    landed(halos[1])

    def unpack_y(q, carry):
        lane = iota((32, 128), 1) < 64
        left, right = hl[q], hr[q]
        pairs = (
            jnp.where(lane, right, pltpu.roll(left, 64, 1)),
            jnp.where(lane, pltpu.roll(right, 64, 1), left),
        )
        for p in range(32):
            s, z = q * 4 + p // 8, p % 8
            k = 4 * (p % 16)
            both = pairs[p // 16]
            both = pltpu.roll(both, 128 - k, 1) if k else both
            both = jnp.concatenate([both[0:8], both[24:32], both[8:24]], axis=0)
            hi, lo = split(both)
            cs[s, z, :, 512:640] = hi
            cs[s, z, :, 640:768] = lo
        return carry

    lax.fori_loop(0, 4, unpack_y, 0)

    def step(half, z):
        kept = 0 if half == 1 else 16
        sources = []
        for t in range(2):
            r0 = ROWS[half][t]
            minus = -1.0 / temp[z, r0 : r0 + 8, :]
            for k in range(NR // 2):
                if k % 8 == 0:
                    pass
                rates = []
                for r in (2 * k, 2 * k + 1):
                    product = c[r % NS, z, r0 : r0 + 8, :] * c[(3 * r + 1) % NS, z, r0 : r0 + 8, :]
                    rates.append(jnp.exp(act_ref[r] * minus) * product)
                hi, lo = split(jnp.concatenate(rates, axis=0))
                rhi[t, 16 * k : 16 * k + 16, :] = hi
                rlo[t, 16 * k : 16 * k + 16, :] = lo
            both = dot(w2[...], rhi[t])
            sources.append(both[0:128] + both[128:256] + dot(w2[0:128], rlo[t]))
        if half == 1:
            ghost = jnp.concatenate([hp[z].reshape(64, 256), hn[z].reshape(64, 256)], axis=0)
            ghost = jnp.concatenate(split(ghost), axis=0)
        for b in range(2):
            sb = slice(8 * b, 8 * b + 8)
            oy = dot(cs[sb, z, kept : kept + 16, :].reshape(128, 768), by[...])
            field = jnp.concatenate(
                [cs[sb, z, :, 0:256].reshape(256, 256), cs[sb, z, :, 256:512].reshape(256, 256)], axis=0
            )
            ox = dot(am[half], field)
            if half == 1:
                ox = ox + dot(ah[b], ghost)
            oy = oy.reshape(8, 16, 512)
            ox1, ox2 = ox[0:128].reshape(8, 16, 256), ox[128:256].reshape(8, 16, 256)
            tiles = []
            for t in range(2):
                r0 = ROWS[half][t]
                rt = slice(8 * t, 8 * t + 8)
                fx = vx[z, r0 : r0 + 8, :] * K_X
                fy = vy[z, r0 : r0 + 8, :] * K_X
                new = c[sb, z, r0 : r0 + 8, :] * CENTRE + sources[t].reshape(16, 8, 256)[sb]
                new = new + (ox2[:, rt] + oy[:, rt, 256:512]) * K_2
                new = new + fx * ox1[:, rt] + fy * oy[:, rt, 0:256]
                out_ref[sb, z, r0 : r0 + 8, :] = new
                tiles.append(new)
            hi, lo = split(jnp.concatenate(tiles, axis=1).reshape(128, 256))
            nhi[128 * b : 128 * b + 128, :] = hi
            nlo[128 * b : 128 * b + 128, :] = lo
        both = dot(vt2[...], nhi[...], ((1,), (1,)))
        total = both[0:64] + both[64:128] + dot(vt2[0:64], nlo[...], ((1,), (1,)))
        part[:, half, z] = total.reshape(8, 8, 256)

    def send_part(half, zg, d):
        chunk = 2 * half + zg
        zs = pl.ds(4 * zg, 4)
        return pltpu.make_async_remote_copy(
            part.at[gy_peer[d], half, zs],
            got.at[d - 1, half, zs],
            part_send.at[chunk, d - 1],
            part_recv.at[chunk, d - 1],
            device_id={"gx": mx, "gy": gy_peer[d]},
            device_id_type=MESH,
        )

    for half in range(2):
        if half == 1:
            landed(halos[2])
            landed(halos[3])

        def group(zg, carry, half=half):
            def one(k, inner):
                step(half, 4 * zg + k)
                return inner

            lax.fori_loop(0, 4, one, 0)
            if remote:
                for d in range(1, ngy):
                    send_part(half, zg, d).start()
            return carry

        lax.fori_loop(0, 2, group, 0)

    if remote:
        for half in range(2):
            for zg in range(2):
                for d in range(1, ngy):
                    send_part(half, zg, d).wait_recv()
    mine = my if remote else 0
    for half in range(2):
        total = part[mine, half].reshape(64, 256)
        if remote:
            for d in range(1, ngy):
                total = total + got[d - 1, half].reshape(64, 256)
        hi, lo = split(total)
        for h in range(2):
            yhi[64 * h : 64 * h + 64, 128 * half : 128 * half + 128] = hi[:, 128 * h : 128 * h + 128]
            ylo[64 * h : 64 * h + 64, 128 * half : 128 * half + 128] = lo[:, 128 * h : 128 * h + 128]
    both = dot(xb2[...], yhi[...], ((1,), (1,)))
    total = both[0:512] + both[512:1024] + dot(xb2[0:512], ylo[...], ((1,), (1,)))
    g[...] = total.reshape(2, 16, 2, 8, 128)

    if remote:
        pair = pltpu.make_async_remote_copy(
            g.at[1 - par],
            pair_got,
            pair_sems.at[0],
            pair_sems.at[1],
            device_id={"gx": partner, "gy": my},
            device_id_type=MESH,
        )
        pair.start()
        pair.wait_recv()
        gs[...] = g[par] + pair_got[...]
        spread_out = []
        for d in range(1, ngx // 2):
            copy = pltpu.make_async_remote_copy(
                gs.at[chip_peer[d]],
                core_got.at[d - 1],
                core_send.at[d - 1],
                core_recv.at[d - 1],
                device_id={"gx": 2 * chip_peer[d] + par, "gy": my},
                device_id_type=MESH,
            )
            copy.start()
            spread_out.append(copy)
        total = gs[chip]
        for d, copy in enumerate(spread_out):
            copy.wait_recv()
            total = total + core_got[d]
    else:
        total = g[0, 0]

    a, b = iota((128, 128), 0), iota((128, 128), 1)
    swap = (a == b // 64 * 64 + b % 8 * 8 + b % 64 // 8).astype(F32)
    total = dot(total.reshape(16, 128), swap, precision=HIGHEST).reshape(2, 8, 128)
    sub, lane = iota((8, 128), 0), iota((8, 128), 1) % 64 // 8
    for i in range(2):
        tile = total[i]
        result = jnp.zeros((8, 128), F32)
        for d in range(8):
            turned = pltpu.roll(tile, d, 0) if d else tile
            if d:
                turned = jnp.where(
                    lane + d < 8, pltpu.roll(turned, 128 - 8 * d, 1), pltpu.roll(turned, 64 - 8 * d, 1)
                )
            result = jnp.where(lane == (sub - d + 8) % 8, turned, result)
        core_ref[i] = result

    if remote:
        for copy in halos:
            copy.wait_send()
        for half in range(2):
            for zg in range(2):
                for d in range(1, ngy):
                    send_part(half, zg, d).wait_send()
        pair.wait_send()
        for copy in spread_out:
            copy.wait_send()


def section(c, vx, vy, temp, pref, act, stoich, load_x, load_y, remote=True, ngx=32, ngy=8):
    vmem = pl.BlockSpec(memory_space=pltpu.VMEM)
    smem = pl.BlockSpec(memory_space=pltpu.SMEM)
    hbm = pl.BlockSpec(memory_space=pl.ANY)
    scratch = [
        pltpu.VMEM((NS, NZ, CX, CY_), F32),
        pltpu.VMEM((NZ, CX, CY_), F32),
        pltpu.VMEM((NZ, CX, CY_), F32),
        pltpu.VMEM((NZ, CX, CY_), F32),
        pltpu.VMEM(BY.shape, BF16),
        pltpu.VMEM(AMAIN.shape, BF16),
        pltpu.VMEM(AHALO.shape, BF16),
        pltpu.VMEM((NS, NZ, CX, 768), BF16),
        pltpu.VMEM((NZ, 8, 8, CY_), F32),
        pltpu.VMEM((NZ, 8, 8, CY_), F32),
        pltpu.VMEM((NZ, 8, 8, CY_), F32),
        pltpu.VMEM((NZ, 8, 8, CY_), F32),
        pltpu.VMEM((4, CX, 128), F32),
        pltpu.VMEM((4, CX, 128), F32),
        pltpu.VMEM((4, CX, 128), F32),
        pltpu.VMEM((4, CX, 128), F32),
        pltpu.VMEM((256, 256), BF16),
        pltpu.VMEM((128, 256), BF16),
        pltpu.VMEM((1024, 256), BF16),
        pltpu.VMEM((2, 256, 256), BF16),
        pltpu.VMEM((2, 256, 256), BF16),
        pltpu.VMEM((256, 256), BF16),
        pltpu.VMEM((256, 256), BF16),
        pltpu.VMEM((8, 2, NZ, 8, 256), F32),
        pltpu.VMEM((7, 2, NZ, 8, 256), F32),
        pltpu.VMEM((128, 256), BF16),
        pltpu.VMEM((128, 256), BF16),
        pltpu.VMEM((2, 16, 2, 8, 128), F32),
        pltpu.VMEM((16, 2, 8, 128), F32),
        pltpu.VMEM((16, 2, 8, 128), F32),
        pltpu.VMEM((15, 2, 8, 128), F32),
        pltpu.SemaphoreType.DMA((NZ + 6,)),
        pltpu.SemaphoreType.DMA((4,)),
        pltpu.SemaphoreType.DMA((4,)),
        pltpu.SemaphoreType.DMA((4, 7)),
        pltpu.SemaphoreType.DMA((4, 7)),
        pltpu.SemaphoreType.DMA((2,)),
        pltpu.SemaphoreType.DMA((15,)),
        pltpu.SemaphoreType.DMA((15,)),
    ]
    params = dict(vmem_limit_bytes=60 * 1024 * 1024)
    if remote:
        params.update(collective_id=0, has_side_effects=True)
    return pl.pallas_call(
        functools.partial(kernel, remote, ngx, ngy),
        name="section",
        out_shape=(
            jax.ShapeDtypeStruct((NS, NZ, CX, CY_), F32),
            jax.ShapeDtypeStruct((2, 8, 128), F32),
        ),
        in_specs=[smem, vmem, vmem, vmem, vmem] + [hbm] * 7,
        out_specs=(vmem, vmem),
        scratch_shapes=scratch,
        compiler_params=pltpu.CompilerParams(**params),
    )(
        act,
        pref.reshape(1, NR),
        stoich,
        load_x,
        load_y,
        c,
        vx,
        vy,
        temp,
        jnp.asarray(BY),
        jnp.asarray(AMAIN),
        jnp.asarray(AHALO),
    )


def solution(mesh):
    in_specs = (
        P(None, None, "gx", "gy"),
        P(None, "gx", "gy"),
        P(None, "gx", "gy"),
        P(None, "gx", "gy"),
        P(),
        P(),
        P(),
        P("gx", None),
        P("gy", None),
    )
    out_specs = (P(None, None, "gx", "gy"), P("gx", "gy", None))
    body = functools.partial(section, ngx=mesh.shape["gx"], ngy=mesh.shape["gy"])
    return jax.shard_map(body, mesh=mesh, in_specs=in_specs, out_specs=out_specs, check_vma=False)
```

```python
import functools
import jax
import jax.numpy as jnp
import numpy as np
import ml_dtypes
from jax import lax
from jax.experimental import pallas as pl
from jax.experimental.pallas import tpu as pltpu
from jax.sharding import PartitionSpec as P

NS, NR, NZ = 16, 32, 8
CX, CY_ = 32, 256
RANK = 64
STEP, DIFF = 0.5, 0.2
SCALE_1, SCALE_2 = 840, 5040
D1 = (672, -168, 32, -3)
D2 = (8064, -1008, 128, -9)
CENTRE = 1.0 + STEP * DIFF * 2.0 * (-205.0 / 72.0)
K_X = -STEP / SCALE_1
K_2 = STEP * DIFF / SCALE_2
F32, BF16 = jnp.float32, jnp.bfloat16
MESH = pl.DeviceIdType.MESH
HIGHEST = lax.Precision.HIGHEST
ROWS = ((8, 16), (0, 24))
X_OF = [list(range(8, 24)), list(range(0, 8)) + list(range(24, 32))]
KEPT = X_OF[1] + X_OF[0]


def tap(kind, offset):
    if offset == 0 or abs(offset) > 4:
        return 0
    if kind == 0:
        return D1[abs(offset) - 1] * (1 if offset > 0 else -1)
    return D2[abs(offset) - 1]


def stencil_tables():
    by = np.zeros((384, 512), np.float32)
    for kind in range(2):
        for out in range(256):
            for off in range(-4, 5):
                y = out + off
                row = y if 0 <= y < 256 else (256 + (y - 256) if y >= 256 else 256 + 64 + (y + 4))
                by[row, kind * 256 + out] = tap(kind, off)
    by = np.concatenate([by[:256], by[:256], by[256:], by[256:]], axis=0)
    main = np.zeros((2, 256, 256), np.float32)
    halo = np.zeros((2, 256, 128), np.float32)
    for half in range(2):
        for kind in range(2):
            for s in range(8):
                for i, x in enumerate(X_OF[half]):
                    row = kind * 128 + s * 16 + i
                    for k, xx in enumerate(KEPT):
                        main[half, row, s * 32 + k] = tap(kind, xx - x)
    for block in range(2):
        for kind in range(2):
            for s in range(8):
                for i, x in enumerate(X_OF[1]):
                    row = kind * 128 + s * 16 + i
                    for k in range(4):
                        halo[block, row, s * 8 + block * 4 + k] = tap(kind, (k - 4) - x)
                        halo[block, row, 64 + s * 8 + block * 4 + k] = tap(kind, (32 + k) - x)
    main = np.concatenate([main, main], axis=2)
    halo = np.concatenate([halo, halo], axis=2)
    bf = ml_dtypes.bfloat16
    return by.astype(bf), main.astype(bf), halo.astype(bf)


BY, AMAIN, AHALO = stencil_tables()


def split(x):
    hi = x.astype(BF16)
    return hi, (x - hi.astype(F32)).astype(BF16)


def dot(a, b, dims=((1,), (0,)), precision=None):
    return lax.dot_general(a, b, (dims, ((), ())), precision=precision, preferred_element_type=F32)


def iota(shape, dim):
    return lax.broadcasted_iota(jnp.int32, shape, dim)


def kernel(
    remote,
    ngx,
    ngy,
    act_ref,
    pref_ref,
    stoich_ref,
    load_x_ref,
    load_y_ref,
    c_hbm,
    vx_hbm,
    vy_hbm,
    t_hbm,
    by_hbm,
    am_hbm,
    ah_hbm,
    out_ref,
    core_ref,
    c,
    vx,
    vy,
    temp,
    by,
    am,
    ah,
    cs,
    xn,
    xp,
    hp,
    hn,
    yl,
    yr,
    hl,
    hr,
    w2,
    vt2,
    xb2,
    rhi,
    rlo,
    nhi,
    nlo,
    part,
    got,
    yhi,
    ylo,
    g,
    pair_got,
    gs,
    core_got,
    load_sems,
    halo_send,
    halo_recv,
    part_send,
    part_recv,
    pair_sems,
    core_send,
    core_recv,
):
    loads = []
    for k in range(NZ):
        loads.append(pltpu.make_async_copy(c_hbm.at[:, k], c.at[:, k], load_sems.at[k]))
    for k, (src, dst) in enumerate(((vx_hbm, vx), (vy_hbm, vy), (t_hbm, temp), (by_hbm, by), (am_hbm, am), (ah_hbm, ah))):
        loads.append(pltpu.make_async_copy(src, dst, load_sems.at[NZ + k]))
    for copy in loads:
        copy.start()
    if remote:
        mx, my = lax.axis_index("gx"), lax.axis_index("gy")
        par = lax.rem(mx, 2)
        chip = mx // 2
        barrier = pltpu.get_barrier_semaphore()
        gy_peer = [lax.rem(my + d, ngy) for d in range(ngy)]
        chip_peer = [lax.rem(chip + d, ngx // 2) for d in range(ngx // 2)]
        partner = mx + 1 - 2 * par
        other = lax.rem(mx + 2 * par - 1 + ngx, ngx)
        for d in range(1, ngy):
            pl.semaphore_signal(barrier, inc=1, device_id={"gx": mx, "gy": gy_peer[d]}, device_id_type=MESH)
        for d in range(1, ngx // 2):
            pl.semaphore_signal(barrier, inc=1, device_id={"gx": 2 * chip_peer[d] + par, "gy": my}, device_id_type=MESH)
        for to in (partner, other):
            pl.semaphore_signal(barrier, inc=1, device_id={"gx": to, "gy": my}, device_id_type=MESH)

    fold = dot((iota((128, 16), 0) // 8 == iota((128, 16), 1)).astype(F32), stoich_ref[...], precision=HIGHEST)
    widen = (iota((32, 256), 1) // 8 == iota((32, 256), 0)).astype(F32)
    table = dot(fold, widen, precision=HIGHEST)
    scale = dot(jnp.broadcast_to(pref_ref[...], (8, 32)), widen, precision=HIGHEST)[0:1] * STEP
    table = jnp.where(iota((128, 256), 0) % 8 == iota((128, 256), 1) % 8, table * scale, 0.0)
    hi, lo = split(table)
    w2[0:128], w2[128:256] = hi, lo
    hi, lo = split(load_y_ref[...])
    vt2[0:64], vt2[64:128] = hi, lo
    row = iota((512, 64), 0) // 8
    rank = 4 * (row % 32 // 2) + 2 * (row // 32) + row % 2
    pick = (rank == iota((512, 64), 1)).astype(F32)
    col = iota((32, 256), 1)
    kept = col // 128 * 16 + col % 16
    x_of = jnp.where(kept < 16, 8 + kept, jnp.where(kept < 24, kept - 16, kept))
    spread = (x_of == iota((32, 256), 0)).astype(F32)
    wide = dot(load_x_ref[...], spread, ((0,), (0,)), HIGHEST)
    wide = dot(pick, wide, precision=HIGHEST)
    wide = jnp.where(iota((512, 256), 0) % 8 == iota((512, 256), 1) % 128 // 16, wide, 0.0)
    hi, lo = split(wide)
    xb2[0:512], xb2[512:1024] = hi, lo

    for copy in loads[:NZ]:
        copy.wait()

    def pack_y(q, carry):
        lane = iota((32, 128), 1) // 4
        left = jnp.zeros((32, 128), F32)
        right = jnp.zeros((32, 128), F32)
        for p in range(32):
            s, z = q * 4 + p // 8, p % 8
            first, last = c[s, z, :, 0:128], c[s, z, :, 128:256]
            left = jnp.where(lane == p, pltpu.roll(first, 4 * p, 1) if p else first, left)
            right = jnp.where(lane == p, pltpu.roll(last, (4 * p + 4) % 128, 1) if p < 31 else last, right)
        yl[q], yr[q] = left, right
        return carry

    lax.fori_loop(0, 4, pack_y, 0)

    def pack_x(z, carry):
        low = iota((8, 256), 0) < 4
        for s in range(8):
            xn[z, s] = jnp.where(low, pltpu.roll(c[s, z, 24:32, :], 4, 0), c[s + 8, z, 24:32, :])
            xp[z, s] = jnp.where(low, c[s, z, 0:8, :], pltpu.roll(c[s + 8, z, 0:8, :], 4, 0))
        return carry

    lax.fori_loop(0, NZ, pack_x, 0)

    if remote:
        pl.semaphore_wait(barrier, ngy - 1 + ngx // 2 - 1 + 2)
        up_x, down_x = lax.rem(mx + 1, ngx), lax.rem(mx + ngx - 1, ngx)
        targets = (
            (yr, hl, mx, gy_peer[1]),
            (yl, hr, mx, gy_peer[ngy - 1]),
            (xn, hp, up_x, my),
            (xp, hn, down_x, my),
        )
        halos = [
            pltpu.make_async_remote_copy(
                src, dst, halo_send.at[k], halo_recv.at[k], device_id={"gx": tx, "gy": ty}, device_id_type=MESH
            )
            for k, (src, dst, tx, ty) in enumerate(targets)
        ]
    else:
        halos = [
            pltpu.make_async_copy(src, dst, halo_recv.at[k])
            for k, (src, dst) in enumerate(((yr, hl), (yl, hr), (xn, hp), (xp, hn)))
        ]
    for copy in halos:
        copy.start()

    def presplit(z, carry):
        for s in range(NS):
            for k, (a, b) in enumerate((ROWS[1], ROWS[0])):
                both = jnp.concatenate([c[s, z, a : a + 8, :], c[s, z, b : b + 8, :]], axis=0)
                hi, lo = split(both)
                cs[s, z, 16 * k : 16 * k + 16, 0:256] = hi
                cs[s, z, 16 * k : 16 * k + 16, 256:512] = lo
        return carry

    lax.fori_loop(0, NZ, presplit, 0)
    for copy in loads[NZ:]:
        copy.wait()

    def landed(copy):
        if remote:
            copy.wait_recv()
        else:
            copy.wait()

    landed(halos[0])
    landed(halos[1])

    def unpack_y(q, carry):
        lane = iota((32, 128), 1) < 64
        left, right = hl[q], hr[q]
        pairs = (
            jnp.where(lane, right, pltpu.roll(left, 64, 1)),
            jnp.where(lane, pltpu.roll(right, 64, 1), left),
        )
        for p in range(32):
            s, z = q * 4 + p // 8, p % 8
            k = 4 * (p % 16)
            both = pairs[p // 16]
            both = pltpu.roll(both, 128 - k, 1) if k else both
            both = jnp.concatenate([both[0:8], both[24:32], both[8:24]], axis=0)
            hi, lo = split(both)
            cs[s, z, :, 512:640] = hi
            cs[s, z, :, 640:768] = lo
        return carry

    lax.fori_loop(0, 4, unpack_y, 0)

    def step(half, z):
        kept = 0 if half == 1 else 16
        sources = []
        for t in range(2):
            r0 = ROWS[half][t]
            minus = -1.0 / temp[z, r0 : r0 + 8, :]
            for k in range(NR // 2):
                if k % 8 == 0:
                    pass
                rates = []
                for r in (2 * k, 2 * k + 1):
                    product = c[r % NS, z, r0 : r0 + 8, :] * c[(3 * r + 1) % NS, z, r0 : r0 + 8, :]
                    rates.append(jnp.exp(act_ref[r] * minus) * product)
                hi, lo = split(jnp.concatenate(rates, axis=0))
                rhi[t, 16 * k : 16 * k + 16, :] = hi
                rlo[t, 16 * k : 16 * k + 16, :] = lo
            both = dot(w2[...], rhi[t])
            sources.append(both[0:128] + both[128:256] + dot(w2[0:128], rlo[t]))
        if half == 1:
            ghost = jnp.concatenate([hp[z].reshape(64, 256), hn[z].reshape(64, 256)], axis=0)
            ghost = jnp.concatenate(split(ghost), axis=0)
        for b in range(2):
            sb = slice(8 * b, 8 * b + 8)
            oy = dot(cs[sb, z, kept : kept + 16, :].reshape(128, 768), by[...])
            field = jnp.concatenate(
                [cs[sb, z, :, 0:256].reshape(256, 256), cs[sb, z, :, 256:512].reshape(256, 256)], axis=0
            )
            ox = dot(am[half], field)
            if half == 1:
                ox = ox + dot(ah[b], ghost)
            oy = oy.reshape(8, 16, 512)
            ox1, ox2 = ox[0:128].reshape(8, 16, 256), ox[128:256].reshape(8, 16, 256)
            tiles = []
            for t in range(2):
                r0 = ROWS[half][t]
                rt = slice(8 * t, 8 * t + 8)
                fx = vx[z, r0 : r0 + 8, :] * K_X
                fy = vy[z, r0 : r0 + 8, :] * K_X
                new = c[sb, z, r0 : r0 + 8, :] * CENTRE + sources[t].reshape(16, 8, 256)[sb]
                new = new + (ox2[:, rt] + oy[:, rt, 256:512]) * K_2
                new = new + fx * ox1[:, rt] + fy * oy[:, rt, 0:256]
                out_ref[sb, z, r0 : r0 + 8, :] = new
                tiles.append(new)
            hi, lo = split(jnp.concatenate(tiles, axis=1).reshape(128, 256))
            nhi[128 * b : 128 * b + 128, :] = hi
            nlo[128 * b : 128 * b + 128, :] = lo
        both = dot(vt2[...], nhi[...], ((1,), (1,)))
        total = both[0:64] + both[64:128] + dot(vt2[0:64], nlo[...], ((1,), (1,)))
        part[:, half, z] = total.reshape(8, 8, 256)

    def send_part(half, zg, d):
        chunk = 2 * half + zg
        zs = pl.ds(4 * zg, 4)
        return pltpu.make_async_remote_copy(
            part.at[gy_peer[d], half, zs],
            got.at[d - 1, half, zs],
            part_send.at[chunk, d - 1],
            part_recv.at[chunk, d - 1],
            device_id={"gx": mx, "gy": gy_peer[d]},
            device_id_type=MESH,
        )

    for half in range(2):
        if half == 1:
            landed(halos[2])
            landed(halos[3])

        def group(zg, carry, half=half):
            def one(k, inner):
                step(half, 4 * zg + k)
                return inner

            lax.fori_loop(0, 4, one, 0)
            if remote:
                for d in range(1, ngy):
                    send_part(half, zg, d).start()
            return carry

        lax.fori_loop(0, 2, group, 0)

    if remote:
        for half in range(2):
            for zg in range(2):
                for d in range(1, ngy):
                    send_part(half, zg, d).wait_recv()
    mine = my if remote else 0
    for half in range(2):
        total = part[mine, half].reshape(64, 256)
        if remote:
            for d in range(1, ngy):
                total = total + got[d - 1, half].reshape(64, 256)
        hi, lo = split(total)
        for h in range(2):
            yhi[64 * h : 64 * h + 64, 128 * half : 128 * half + 128] = hi[:, 128 * h : 128 * h + 128]
            ylo[64 * h : 64 * h + 64, 128 * half : 128 * half + 128] = lo[:, 128 * h : 128 * h + 128]
    both = dot(xb2[...], yhi[...], ((1,), (1,)))
    total = both[0:512] + both[512:1024] + dot(xb2[0:512], ylo[...], ((1,), (1,)))
    g[...] = total.reshape(2, 16, 2, 8, 128)

    if remote:
        pair = pltpu.make_async_remote_copy(
            g.at[1 - par],
            pair_got,
            pair_sems.at[0],
            pair_sems.at[1],
            device_id={"gx": partner, "gy": my},
            device_id_type=MESH,
        )
        pair.start()
        pair.wait_recv()
        gs[...] = g[par] + pair_got[...]
        spread_out = []
        for d in range(1, ngx // 2):
            copy = pltpu.make_async_remote_copy(
                gs.at[chip_peer[d]],
                core_got.at[d - 1],
                core_send.at[d - 1],
                core_recv.at[d - 1],
                device_id={"gx": 2 * chip_peer[d] + par, "gy": my},
                device_id_type=MESH,
            )
            copy.start()
            spread_out.append(copy)
        total = gs[chip]
        for d, copy in enumerate(spread_out):
            copy.wait_recv()
            total = total + core_got[d]
    else:
        total = g[0, 0]

    a, b = iota((128, 128), 0), iota((128, 128), 1)
    swap = (a == b // 64 * 64 + b % 8 * 8 + b % 64 // 8).astype(F32)
    total = dot(total.reshape(16, 128), swap, precision=HIGHEST).reshape(2, 8, 128)
    sub, lane = iota((8, 128), 0), iota((8, 128), 1) % 64 // 8
    for i in range(2):
        tile = total[i]
        result = jnp.zeros((8, 128), F32)
        for d in range(8):
            turned = pltpu.roll(tile, d, 0) if d else tile
            if d:
                turned = jnp.where(
                    lane + d < 8, pltpu.roll(turned, 128 - 8 * d, 1), pltpu.roll(turned, 64 - 8 * d, 1)
                )
            result = jnp.where(lane == (sub - d + 8) % 8, turned, result)
        core_ref[i] = result

    if remote:
        for copy in halos:
            copy.wait_send()
        for half in range(2):
            for zg in range(2):
                for d in range(1, ngy):
                    send_part(half, zg, d).wait_send()
        pair.wait_send()
        for copy in spread_out:
            copy.wait_send()


def section(c, vx, vy, temp, pref, act, stoich, load_x, load_y, remote=True, ngx=32, ngy=8):
    vmem = pl.BlockSpec(memory_space=pltpu.VMEM)
    smem = pl.BlockSpec(memory_space=pltpu.SMEM)
    hbm = pl.BlockSpec(memory_space=pltpu.HBM)
    scratch = [
        pltpu.VMEM((NS, NZ, CX, CY_), F32),
        pltpu.VMEM((NZ, CX, CY_), F32),
        pltpu.VMEM((NZ, CX, CY_), F32),
        pltpu.VMEM((NZ, CX, CY_), F32),
        pltpu.VMEM(BY.shape, BF16),
        pltpu.VMEM(AMAIN.shape, BF16),
        pltpu.VMEM(AHALO.shape, BF16),
        pltpu.VMEM((NS, NZ, CX, 768), BF16),
        pltpu.VMEM((NZ, 8, 8, CY_), F32),
        pltpu.VMEM((NZ, 8, 8, CY_), F32),
        pltpu.VMEM((NZ, 8, 8, CY_), F32),
        pltpu.VMEM((NZ, 8, 8, CY_), F32),
        pltpu.VMEM((4, CX, 128), F32),
        pltpu.VMEM((4, CX, 128), F32),
        pltpu.VMEM((4, CX, 128), F32),
        pltpu.VMEM((4, CX, 128), F32),
        pltpu.VMEM((256, 256), BF16),
        pltpu.VMEM((128, 256), BF16),
        pltpu.VMEM((1024, 256), BF16),
        pltpu.VMEM((2, 256, 256), BF16),
        pltpu.VMEM((2, 256, 256), BF16),
        pltpu.VMEM((256, 256), BF16),
        pltpu.VMEM((256, 256), BF16),
        pltpu.VMEM((8, 2, NZ, 8, 256), F32),
        pltpu.VMEM((7, 2, NZ, 8, 256), F32),
        pltpu.VMEM((128, 256), BF16),
        pltpu.VMEM((128, 256), BF16),
        pltpu.VMEM((2, 16, 2, 8, 128), F32),
        pltpu.VMEM((16, 2, 8, 128), F32),
        pltpu.VMEM((16, 2, 8, 128), F32),
        pltpu.VMEM((15, 2, 8, 128), F32),
        pltpu.SemaphoreType.DMA((NZ + 6,)),
        pltpu.SemaphoreType.DMA((4,)),
        pltpu.SemaphoreType.DMA((4,)),
        pltpu.SemaphoreType.DMA((4, 7)),
        pltpu.SemaphoreType.DMA((4, 7)),
        pltpu.SemaphoreType.DMA((2,)),
        pltpu.SemaphoreType.DMA((15,)),
        pltpu.SemaphoreType.DMA((15,)),
    ]
    params = dict(vmem_limit_bytes=59 * 1024 * 1024)
    if remote:
        params.update(collective_id=0, has_side_effects=True)
    return pl.pallas_call(
        functools.partial(kernel, remote, ngx, ngy),
        name="section",
        out_shape=(
            pltpu.VMEM((NS, NZ, CX, CY_), F32),
            pltpu.VMEM((2, 8, 128), F32),
        ),
        in_specs=[smem, vmem, vmem, vmem, vmem] + [hbm] * 7,
        out_specs=(vmem, vmem),
        scratch_shapes=scratch,
        compiler_params=pltpu.CompilerParams(**params),
    )(
        act,
        pref.reshape(1, NR),
        stoich.T,
        load_x,
        load_y.T,
        c,
        vx,
        vy,
        temp,
        jnp.asarray(BY),
        jnp.asarray(AMAIN),
        jnp.asarray(AHALO),
    )


def solution(mesh):
    in_specs = (
        P(None, None, "gx", "gy"),
        P(None, "gx", "gy"),
        P(None, "gx", "gy"),
        P(None, "gx", "gy"),
        P(),
        P(),
        P(),
        P("gx", None),
        P("gy", None),
    )
    out_specs = (P(None, None, "gx", "gy"), P("gx", "gy", None))
    body = functools.partial(section, ngx=mesh.shape["gx"], ngy=mesh.shape["gy"])
    return jax.shard_map(body, mesh=mesh, in_specs=in_specs, out_specs=out_specs, check_vma=False)
```

```python
import functools
import jax
import jax.numpy as jnp
import numpy as np
import ml_dtypes
from jax import lax
from jax.experimental import pallas as pl
from jax.experimental.pallas import tpu as pltpu
from jax.sharding import PartitionSpec as P

NS, NR, NZ = 16, 32, 8
CX, CY_ = 32, 256
RANK = 64
STEP, DIFF = 0.5, 0.2
SCALE_1, SCALE_2 = 840, 5040
D1 = (672, -168, 32, -3)
D2 = (8064, -1008, 128, -9)
CENTRE = 1.0 + STEP * DIFF * 2.0 * (-205.0 / 72.0)
K_X = -STEP / SCALE_1
K_2 = STEP * DIFF / SCALE_2
F32, BF16 = jnp.float32, jnp.bfloat16
MESH = pl.DeviceIdType.MESH
HIGHEST = lax.Precision.HIGHEST
ROWS = ((8, 16), (0, 24))
X_OF = [list(range(8, 24)), list(range(0, 8)) + list(range(24, 32))]
KEPT = X_OF[1] + X_OF[0]
GY_ORDER = sorted(range(1, 8), key=lambda d: -(d // 4 + min(d % 4, 4 - d % 4)))
GX_ORDER = sorted(range(1, 16), key=lambda d: -(2 * (d // 8) + min(d % 8, 8 - d % 8)))


def tap(kind, offset):
    if offset == 0 or abs(offset) > 4:
        return 0
    if kind == 0:
        return D1[abs(offset) - 1] * (1 if offset > 0 else -1)
    return D2[abs(offset) - 1]


def stencil_tables():
    by = np.zeros((384, 512), np.float32)
    for kind in range(2):
        for out in range(256):
            for off in range(-4, 5):
                y = out + off
                row = y if 0 <= y < 256 else (256 + (y - 256) if y >= 256 else 256 + 64 + (y + 4))
                by[row, kind * 256 + out] = tap(kind, off)
    by = np.concatenate([by[:256], by[:256], by[256:], by[256:]], axis=0)
    main = np.zeros((2, 256, 256), np.float32)
    halo = np.zeros((2, 256, 128), np.float32)
    for half in range(2):
        for kind in range(2):
            for s in range(8):
                for i, x in enumerate(X_OF[half]):
                    row = kind * 128 + s * 16 + i
                    for k, xx in enumerate(KEPT):
                        main[half, row, s * 32 + k] = tap(kind, xx - x)
    for block in range(2):
        for kind in range(2):
            for s in range(8):
                for i, x in enumerate(X_OF[1]):
                    row = kind * 128 + s * 16 + i
                    for k in range(4):
                        halo[block, row, s * 8 + block * 4 + k] = tap(kind, (k - 4) - x)
                        halo[block, row, 64 + s * 8 + block * 4 + k] = tap(kind, (32 + k) - x)
    main = np.concatenate([main, main], axis=2)
    halo = np.concatenate([halo, halo], axis=2)
    bf = ml_dtypes.bfloat16
    return by.astype(bf), main.astype(bf), halo.astype(bf)


BY, AMAIN, AHALO = stencil_tables()


def split(x):
    hi = x.astype(BF16)
    return hi, (x - hi.astype(F32)).astype(BF16)


def dot(a, b, dims=((1,), (0,)), precision=None):
    return lax.dot_general(a, b, (dims, ((), ())), precision=precision, preferred_element_type=F32)


def iota(shape, dim):
    return lax.broadcasted_iota(jnp.int32, shape, dim)


def kernel(
    remote,
    ngx,
    ngy,
    act_ref,
    pref_ref,
    stoich_ref,
    load_x_ref,
    load_y_ref,
    c_hbm,
    vx_hbm,
    vy_hbm,
    t_hbm,
    by_hbm,
    am_hbm,
    ah_hbm,
    out_ref,
    core_ref,
    c,
    vx,
    vy,
    temp,
    by,
    am,
    ah,
    cs,
    xn,
    xp,
    hp,
    hn,
    yl,
    yr,
    hl,
    hr,
    w2,
    vt2,
    xb2,
    rhi,
    rlo,
    nhi,
    nlo,
    part,
    got,
    yhi,
    ylo,
    g,
    pair_got,
    gs,
    core_got,
    load_sems,
    halo_send,
    halo_recv,
    part_send,
    part_recv,
    pair_sems,
    core_send,
    core_recv,
):
    loads = []
    for k in range(NZ):
        loads.append(pltpu.make_async_copy(c_hbm.at[:, k], c.at[:, k], load_sems.at[k]))
    for k, (src, dst) in enumerate(((vx_hbm, vx), (vy_hbm, vy), (t_hbm, temp), (by_hbm, by), (am_hbm, am), (ah_hbm, ah))):
        loads.append(pltpu.make_async_copy(src, dst, load_sems.at[NZ + k]))
    for copy in loads:
        copy.start()
    if remote:
        mx, my = lax.axis_index("gx"), lax.axis_index("gy")
        par = lax.rem(mx, 2)
        chip = mx // 2
        barrier = pltpu.get_barrier_semaphore()
        gy_peer = [lax.rem(my // 4 + f, 2) * 4 + lax.rem(my + k, 4) for f in range(2) for k in range(4)]
        chip_peer = [lax.rem(chip // 8 + f, 2) * 8 + lax.rem(chip + k, 8) for f in range(2) for k in range(8)]
        partner = mx + 1 - 2 * par
        other = lax.rem(mx + 2 * par - 1 + ngx, ngx)
        for d in range(1, ngy):
            pl.semaphore_signal(barrier, inc=1, device_id={"gx": mx, "gy": gy_peer[d]}, device_id_type=MESH)
        for d in range(1, ngx // 2):
            pl.semaphore_signal(barrier, inc=1, device_id={"gx": 2 * chip_peer[d] + par, "gy": my}, device_id_type=MESH)
        for to in (partner, other):
            pl.semaphore_signal(barrier, inc=1, device_id={"gx": to, "gy": my}, device_id_type=MESH)

    fold = dot((iota((128, 16), 0) // 8 == iota((128, 16), 1)).astype(F32), stoich_ref[...], precision=HIGHEST)
    widen = (iota((32, 256), 1) // 8 == iota((32, 256), 0)).astype(F32)
    table = dot(fold, widen, precision=HIGHEST)
    scale = dot(jnp.broadcast_to(pref_ref[...], (8, 32)), widen, precision=HIGHEST)[0:1] * STEP
    table = jnp.where(iota((128, 256), 0) % 8 == iota((128, 256), 1) % 8, table * scale, 0.0)
    hi, lo = split(table)
    w2[0:128], w2[128:256] = hi, lo
    hi, lo = split(load_y_ref[...])
    vt2[0:64], vt2[64:128] = hi, lo
    row = iota((512, 64), 0) // 8
    rank = 4 * (row % 32 // 2) + 2 * (row // 32) + row % 2
    pick = (rank == iota((512, 64), 1)).astype(F32)
    col = iota((32, 256), 1)
    kept = col // 128 * 16 + col % 16
    x_of = jnp.where(kept < 16, 8 + kept, jnp.where(kept < 24, kept - 16, kept))
    spread = (x_of == iota((32, 256), 0)).astype(F32)
    wide = dot(load_x_ref[...], spread, ((0,), (0,)), HIGHEST)
    wide = dot(pick, wide, precision=HIGHEST)
    wide = jnp.where(iota((512, 256), 0) % 8 == iota((512, 256), 1) % 128 // 16, wide, 0.0)
    hi, lo = split(wide)
    xb2[0:512], xb2[512:1024] = hi, lo

    for copy in loads[:NZ]:
        copy.wait()

    def pack_y(q, carry):
        lane = iota((32, 128), 1) // 4
        left = jnp.zeros((32, 128), F32)
        right = jnp.zeros((32, 128), F32)
        for p in range(32):
            s, z = q * 4 + p // 8, p % 8
            first, last = c[s, z, :, 0:128], c[s, z, :, 128:256]
            left = jnp.where(lane == p, pltpu.roll(first, 4 * p, 1) if p else first, left)
            right = jnp.where(lane == p, pltpu.roll(last, (4 * p + 4) % 128, 1) if p < 31 else last, right)
        yl[q], yr[q] = left, right
        return carry

    lax.fori_loop(0, 4, pack_y, 0)

    def pack_x(z, carry):
        low = iota((8, 256), 0) < 4
        for s in range(8):
            xn[z, s] = jnp.where(low, pltpu.roll(c[s, z, 24:32, :], 4, 0), c[s + 8, z, 24:32, :])
            xp[z, s] = jnp.where(low, c[s, z, 0:8, :], pltpu.roll(c[s + 8, z, 0:8, :], 4, 0))
        return carry

    lax.fori_loop(0, NZ, pack_x, 0)

    if remote:
        pl.semaphore_wait(barrier, ngy - 1 + ngx // 2 - 1 + 2)
        up_x, down_x = lax.rem(mx + 1, ngx), lax.rem(mx + ngx - 1, ngx)
        def halo(k, zg=None):
            src, dst, tx, ty = (
                (yr, hl, mx, lax.rem(my + 1, ngy)),
                (yl, hr, mx, lax.rem(my + ngy - 1, ngy)),
                (xn, hp, up_x, my),
                (xp, hn, down_x, my),
            )[k]
            slot = k
            if zg is not None:
                zs = pl.ds(2 * zg, 2)
                src, dst, slot = src.at[zs], dst.at[zs], 2 + 4 * (k - 2) + zg
            return pltpu.make_async_remote_copy(
                src, dst, halo_send.at[slot], halo_recv.at[slot], device_id={"gx": tx, "gy": ty}, device_id_type=MESH
            )

    for k in range(2):
        halo(k).start()
    for zg in range(4):
        for k in (2, 3):
            halo(k, zg).start()

    def presplit(z, carry):
        for s in range(NS):
            for k, (a, b) in enumerate((ROWS[1], ROWS[0])):
                both = jnp.concatenate([c[s, z, a : a + 8, :], c[s, z, b : b + 8, :]], axis=0)
                hi, lo = split(both)
                cs[s, z, 16 * k : 16 * k + 16, 0:256] = hi
                cs[s, z, 16 * k : 16 * k + 16, 256:512] = lo
        return carry

    lax.fori_loop(0, NZ, presplit, 0)
    for copy in loads[NZ:]:
        copy.wait()

    halo(0).wait_recv()
    halo(1).wait_recv()

    def unpack_y(q, carry):
        lane = iota((32, 128), 1) < 64
        left, right = hl[q], hr[q]
        pairs = (
            jnp.where(lane, right, pltpu.roll(left, 64, 1)),
            jnp.where(lane, pltpu.roll(right, 64, 1), left),
        )
        for p in range(32):
            s, z = q * 4 + p // 8, p % 8
            k = 4 * (p % 16)
            both = pairs[p // 16]
            both = pltpu.roll(both, 128 - k, 1) if k else both
            both = jnp.concatenate([both[0:8], both[24:32], both[8:24]], axis=0)
            hi, lo = split(both)
            cs[s, z, :, 512:640] = hi
            cs[s, z, :, 640:768] = lo
        return carry

    lax.fori_loop(0, 4, unpack_y, 0)

    def step(half, z):
        kept = 0 if half == 1 else 16
        sources = []
        for t in range(2):
            r0 = ROWS[half][t]
            minus = -1.0 / temp[z, r0 : r0 + 8, :]
            for k in range(NR // 2):
                if k % 8 == 0:
                    pass
                rates = []
                for r in (2 * k, 2 * k + 1):
                    product = c[r % NS, z, r0 : r0 + 8, :] * c[(3 * r + 1) % NS, z, r0 : r0 + 8, :]
                    rates.append(jnp.exp(act_ref[r] * minus) * product)
                hi, lo = split(jnp.concatenate(rates, axis=0))
                rhi[t, 16 * k : 16 * k + 16, :] = hi
                rlo[t, 16 * k : 16 * k + 16, :] = lo
            both = dot(w2[...], rhi[t])
            sources.append(both[0:128] + both[128:256] + dot(w2[0:128], rlo[t]))
        if half == 1:
            ghost = jnp.concatenate([hp[z].reshape(64, 256), hn[z].reshape(64, 256)], axis=0)
            ghost = jnp.concatenate(split(ghost), axis=0)
        for b in range(2):
            sb = slice(8 * b, 8 * b + 8)
            oy = dot(cs[sb, z, kept : kept + 16, :].reshape(128, 768), by[...])
            field = jnp.concatenate(
                [cs[sb, z, :, 0:256].reshape(256, 256), cs[sb, z, :, 256:512].reshape(256, 256)], axis=0
            )
            ox = dot(am[half], field)
            if half == 1:
                ox = ox + dot(ah[b], ghost)
            oy = oy.reshape(8, 16, 512)
            ox1, ox2 = ox[0:128].reshape(8, 16, 256), ox[128:256].reshape(8, 16, 256)
            tiles = []
            for t in range(2):
                r0 = ROWS[half][t]
                rt = slice(8 * t, 8 * t + 8)
                fx = vx[z, r0 : r0 + 8, :] * K_X
                fy = vy[z, r0 : r0 + 8, :] * K_X
                new = c[sb, z, r0 : r0 + 8, :] * CENTRE + sources[t].reshape(16, 8, 256)[sb]
                new = new + (ox2[:, rt] + oy[:, rt, 256:512]) * K_2
                new = new + fx * ox1[:, rt] + fy * oy[:, rt, 0:256]
                out_ref[sb, z, r0 : r0 + 8, :] = new
                tiles.append(new)
            hi, lo = split(jnp.concatenate(tiles, axis=1).reshape(128, 256))
            nhi[128 * b : 128 * b + 128, :] = hi
            nlo[128 * b : 128 * b + 128, :] = lo
        both = dot(vt2[...], nhi[...], ((1,), (1,)))
        total = both[0:64] + both[64:128] + dot(vt2[0:64], nlo[...], ((1,), (1,)))
        part[:, half, z] = total.reshape(8, 8, 256)

    def send_part(half, d, zs=slice(None)):
        return pltpu.make_async_remote_copy(
            part.at[gy_peer[d], half, zs],
            got.at[d - 1, half, zs],
            part_send.at[half, d - 1],
            part_recv.at[half, d - 1],
            device_id={"gx": mx, "gy": gy_peer[d]},
            device_id_type=MESH,
        )

    for half in range(2):

        def group(zg, carry, half=half):
            def one(k, inner):
                step(half, 2 * zg + k)
                return inner

            if half == 1:
                halo(2, zg).wait_recv()
                halo(3, zg).wait_recv()
            lax.fori_loop(0, 2, one, 0)
            for d in GY_ORDER:
                send_part(half, d, pl.ds(2 * zg, 2)).start()
            return carry

        lax.fori_loop(0, 4, group, 0)

    for half in range(2):
        total = part[my, half].reshape(64, 256)
        for d in GY_ORDER[::-1]:
            send_part(half, d).wait_recv()
            total = total + got[d - 1, half].reshape(64, 256)
        hi, lo = split(total)
        for h in range(2):
            yhi[64 * h : 64 * h + 64, 128 * half : 128 * half + 128] = hi[:, 128 * h : 128 * h + 128]
            ylo[64 * h : 64 * h + 64, 128 * half : 128 * half + 128] = lo[:, 128 * h : 128 * h + 128]
    both = dot(xb2[...], yhi[...], ((1,), (1,)))
    total = both[0:512] + both[512:1024] + dot(xb2[0:512], ylo[...], ((1,), (1,)))
    g[...] = total.reshape(2, 16, 2, 8, 128)

    if remote:
        pair = pltpu.make_async_remote_copy(
            g.at[1 - par],
            pair_got,
            pair_sems.at[0],
            pair_sems.at[1],
            device_id={"gx": partner, "gy": my},
            device_id_type=MESH,
        )
        pair.start()
        pair.wait_recv()
        gs[...] = g[par] + pair_got[...]
        spread_out = []
        for d in GX_ORDER:
            copy = pltpu.make_async_remote_copy(
                gs.at[chip_peer[d]],
                core_got.at[d - 1],
                core_send.at[d - 1],
                core_recv.at[d - 1],
                device_id={"gx": 2 * chip_peer[d] + par, "gy": my},
                device_id_type=MESH,
            )
            copy.start()
            spread_out.append(copy)
        total = gs[chip]
        for d, copy in list(zip(GX_ORDER, spread_out))[::-1]:
            copy.wait_recv()
            total = total + core_got[d - 1]
    else:
        total = g[0, 0]

    a, b = iota((128, 128), 0), iota((128, 128), 1)
    swap = (a == b // 64 * 64 + b % 8 * 8 + b % 64 // 8).astype(F32)
    total = dot(total.reshape(16, 128), swap, precision=HIGHEST).reshape(2, 8, 128)
    sub, lane = iota((8, 128), 0), iota((8, 128), 1) % 64 // 8
    for i in range(2):
        tile = total[i]
        result = jnp.zeros((8, 128), F32)
        for d in range(8):
            turned = pltpu.roll(tile, d, 0) if d else tile
            if d:
                turned = jnp.where(
                    lane + d < 8, pltpu.roll(turned, 128 - 8 * d, 1), pltpu.roll(turned, 64 - 8 * d, 1)
                )
            result = jnp.where(lane == (sub - d + 8) % 8, turned, result)
        core_ref[i] = result

    if remote:
        for k in range(2):
            halo(k).wait_send()
        for zg in range(4):
            for k in (2, 3):
                halo(k, zg).wait_send()
        for half in range(2):
            for d in GY_ORDER:
                send_part(half, d).wait_send()
        pair.wait_send()
        for copy in spread_out:
            copy.wait_send()


def section(c, vx, vy, temp, pref, act, stoich, load_x, load_y, remote=True, ngx=32, ngy=8):
    vmem = pl.BlockSpec(memory_space=pltpu.VMEM)
    smem = pl.BlockSpec(memory_space=pltpu.SMEM)
    hbm = pl.BlockSpec(memory_space=pltpu.HBM)
    scratch = [
        pltpu.VMEM((NS, NZ, CX, CY_), F32),
        pltpu.VMEM((NZ, CX, CY_), F32),
        pltpu.VMEM((NZ, CX, CY_), F32),
        pltpu.VMEM((NZ, CX, CY_), F32),
        pltpu.VMEM(BY.shape, BF16),
        pltpu.VMEM(AMAIN.shape, BF16),
        pltpu.VMEM(AHALO.shape, BF16),
        pltpu.VMEM((NS, NZ, CX, 768), BF16),
        pltpu.VMEM((NZ, 8, 8, CY_), F32),
        pltpu.VMEM((NZ, 8, 8, CY_), F32),
        pltpu.VMEM((NZ, 8, 8, CY_), F32),
        pltpu.VMEM((NZ, 8, 8, CY_), F32),
        pltpu.VMEM((4, CX, 128), F32),
        pltpu.VMEM((4, CX, 128), F32),
        pltpu.VMEM((4, CX, 128), F32),
        pltpu.VMEM((4, CX, 128), F32),
        pltpu.VMEM((256, 256), BF16),
        pltpu.VMEM((128, 256), BF16),
        pltpu.VMEM((1024, 256), BF16),
        pltpu.VMEM((2, 256, 256), BF16),
        pltpu.VMEM((2, 256, 256), BF16),
        pltpu.VMEM((256, 256), BF16),
        pltpu.VMEM((256, 256), BF16),
        pltpu.VMEM((8, 2, NZ, 8, 256), F32),
        pltpu.VMEM((7, 2, NZ, 8, 256), F32),
        pltpu.VMEM((128, 256), BF16),
        pltpu.VMEM((128, 256), BF16),
        pltpu.VMEM((2, 16, 2, 8, 128), F32),
        pltpu.VMEM((16, 2, 8, 128), F32),
        pltpu.VMEM((16, 2, 8, 128), F32),
        pltpu.VMEM((15, 2, 8, 128), F32),
        pltpu.SemaphoreType.DMA((NZ + 6,)),
        pltpu.SemaphoreType.DMA((10,)),
        pltpu.SemaphoreType.DMA((10,)),
        pltpu.SemaphoreType.DMA((2, 7)),
        pltpu.SemaphoreType.DMA((2, 7)),
        pltpu.SemaphoreType.DMA((2,)),
        pltpu.SemaphoreType.DMA((15,)),
        pltpu.SemaphoreType.DMA((15,)),
    ]
    params = dict(vmem_limit_bytes=59 * 1024 * 1024)
    if remote:
        params.update(collective_id=0, has_side_effects=True)
    return pl.pallas_call(
        functools.partial(kernel, remote, ngx, ngy),
        name="section",
        out_shape=(
            pltpu.VMEM((NS, NZ, CX, CY_), F32),
            pltpu.VMEM((2, 8, 128), F32),
        ),
        in_specs=[smem, vmem, vmem, vmem, vmem] + [hbm] * 7,
        out_specs=(vmem, vmem),
        scratch_shapes=scratch,
        compiler_params=pltpu.CompilerParams(**params),
    )(
        act,
        pref.reshape(1, NR),
        stoich.T,
        load_x,
        load_y.T,
        c,
        vx,
        vy,
        temp,
        jnp.asarray(BY),
        jnp.asarray(AMAIN),
        jnp.asarray(AHALO),
    )


def solution(mesh):
    in_specs = (
        P(None, None, "gx", "gy"),
        P(None, "gx", "gy"),
        P(None, "gx", "gy"),
        P(None, "gx", "gy"),
        P(),
        P(),
        P(),
        P("gx", None),
        P("gy", None),
    )
    out_specs = (P(None, None, "gx", "gy"), P("gx", "gy", None))
    body = functools.partial(section, ngx=mesh.shape["gx"], ngy=mesh.shape["gy"])
    return jax.shard_map(body, mesh=mesh, in_specs=in_specs, out_specs=out_specs, check_vma=False)
```

```python
import functools
import jax
import jax.numpy as jnp
import numpy as np
import ml_dtypes
from jax import lax
from jax.experimental import pallas as pl
from jax.experimental.pallas import tpu as pltpu
from jax.sharding import PartitionSpec as P

NS, NR, NZ = 16, 32, 8
CX, CY_ = 32, 256
RANK = 64
STEP, DIFF = 0.5, 0.2
SCALE_1, SCALE_2 = 840, 5040
D1 = (672, -168, 32, -3)
D2 = (8064, -1008, 128, -9)
CENTRE = 1.0 + STEP * DIFF * 2.0 * (-205.0 / 72.0)
K_X = -STEP / SCALE_1
K_2 = STEP * DIFF / SCALE_2
F32, BF16 = jnp.float32, jnp.bfloat16
MESH = pl.DeviceIdType.MESH
HIGHEST = lax.Precision.HIGHEST
ROWS = ((8, 16), (0, 24))
X_OF = [list(range(8, 24)), list(range(0, 8)) + list(range(24, 32))]
KEPT = X_OF[1] + X_OF[0]
GY_ORDER = sorted(range(1, 8), key=lambda d: -(d // 4 + min(d % 4, 4 - d % 4)))
GX_ORDER = sorted(range(1, 16), key=lambda d: -(2 * (d // 8) + min(d % 8, 8 - d % 8)))


def tap(kind, offset):
    if offset == 0 or abs(offset) > 4:
        return 0
    if kind == 0:
        return D1[abs(offset) - 1] * (1 if offset > 0 else -1)
    return D2[abs(offset) - 1]


def stencil_tables():
    by = np.zeros((384, 512), np.float32)
    for kind in range(2):
        for out in range(256):
            for off in range(-4, 5):
                y = out + off
                row = y if 0 <= y < 256 else (256 + (y - 256) if y >= 256 else 256 + 64 + (y + 4))
                by[row, kind * 256 + out] = tap(kind, off)
    by = np.concatenate([by[:256], by[:256], by[256:], by[256:]], axis=0)
    main = np.zeros((2, 256, 256), np.float32)
    halo = np.zeros((2, 256, 128), np.float32)
    for half in range(2):
        for kind in range(2):
            for s in range(8):
                for i, x in enumerate(X_OF[half]):
                    row = kind * 128 + s * 16 + i
                    for k, xx in enumerate(KEPT):
                        main[half, row, s * 32 + k] = tap(kind, xx - x)
    for block in range(2):
        for kind in range(2):
            for s in range(8):
                for i, x in enumerate(X_OF[1]):
                    row = kind * 128 + s * 16 + i
                    for k in range(4):
                        halo[block, row, s * 8 + block * 4 + k] = tap(kind, (k - 4) - x)
                        halo[block, row, 64 + s * 8 + block * 4 + k] = tap(kind, (32 + k) - x)
    main = np.concatenate([main, main], axis=2)
    halo = np.concatenate([halo, halo], axis=2)
    bf = ml_dtypes.bfloat16
    return by.astype(bf), main.astype(bf), halo.astype(bf)


BY, AMAIN, AHALO = stencil_tables()


def split(x):
    hi = x.astype(BF16)
    return hi, (x - hi.astype(F32)).astype(BF16)


def dot(a, b, dims=((1,), (0,)), precision=None):
    return lax.dot_general(a, b, (dims, ((), ())), precision=precision, preferred_element_type=F32)


def iota(shape, dim):
    return lax.broadcasted_iota(jnp.int32, shape, dim)


def kernel(
    remote,
    ngx,
    ngy,
    act_ref,
    pref_ref,
    stoich_ref,
    load_x_ref,
    load_y_ref,
    c_hbm,
    vx_hbm,
    vy_hbm,
    t_hbm,
    by_hbm,
    am_hbm,
    ah_hbm,
    out_ref,
    core_ref,
    c,
    vx,
    vy,
    temp,
    by,
    am,
    ah,
    cs,
    xn,
    xp,
    hp,
    hn,
    yl,
    yr,
    hl,
    hr,
    w2,
    vt2,
    xb2,
    rhi,
    rlo,
    nhi,
    nlo,
    part,
    got,
    yhi,
    ylo,
    g,
    pair_got,
    gs,
    core_got,
    load_sems,
    halo_send,
    halo_recv,
    part_send,
    part_recv,
    pair_sems,
    core_send,
    core_recv,
):
    loads = []
    for k in range(NZ):
        loads.append(pltpu.make_async_copy(c_hbm.at[:, k], c.at[:, k], load_sems.at[k]))
    for k, (src, dst) in enumerate(((vx_hbm, vx), (vy_hbm, vy), (t_hbm, temp), (by_hbm, by), (am_hbm, am), (ah_hbm, ah))):
        loads.append(pltpu.make_async_copy(src, dst, load_sems.at[NZ + k]))
    for copy in loads:
        copy.start()
    if remote:
        mx, my = lax.axis_index("gx"), lax.axis_index("gy")
        par = lax.rem(mx, 2)
        chip = mx // 2
        barrier = pltpu.get_barrier_semaphore()
        gy_peer = [lax.rem(my // 4 + f, 2) * 4 + lax.rem(my + k, 4) for f in range(2) for k in range(4)]
        chip_peer = [lax.rem(chip // 8 + f, 2) * 8 + lax.rem(chip + k, 8) for f in range(2) for k in range(8)]
        partner = mx + 1 - 2 * par
        other = lax.rem(mx + 2 * par - 1 + ngx, ngx)
        for d in range(1, ngy):
            pl.semaphore_signal(barrier, inc=1, device_id={"gx": mx, "gy": gy_peer[d]}, device_id_type=MESH)
        for d in range(1, ngx // 2):
            pl.semaphore_signal(barrier, inc=1, device_id={"gx": 2 * chip_peer[d] + par, "gy": my}, device_id_type=MESH)
        for to in (partner, other):
            pl.semaphore_signal(barrier, inc=1, device_id={"gx": to, "gy": my}, device_id_type=MESH)

    fold = dot((iota((128, 16), 0) // 8 == iota((128, 16), 1)).astype(F32), stoich_ref[...], precision=HIGHEST)
    widen = (iota((32, 256), 1) // 8 == iota((32, 256), 0)).astype(F32)
    table = dot(fold, widen, precision=HIGHEST)
    scale = dot(jnp.broadcast_to(pref_ref[...], (8, 32)), widen, precision=HIGHEST)[0:1] * STEP
    table = jnp.where(iota((128, 256), 0) % 8 == iota((128, 256), 1) % 8, table * scale, 0.0)
    hi, lo = split(table)
    w2[0:128], w2[128:256] = hi, lo
    hi, lo = split(load_y_ref[...])
    vt2[0:64], vt2[64:128] = hi, lo
    row = iota((512, 64), 0) // 8
    rank = 4 * (row % 32 // 2) + 2 * (row // 32) + row % 2
    pick = (rank == iota((512, 64), 1)).astype(F32)
    col = iota((32, 256), 1)
    kept = col // 128 * 16 + col % 16
    x_of = jnp.where(kept < 16, 8 + kept, jnp.where(kept < 24, kept - 16, kept))
    spread = (x_of == iota((32, 256), 0)).astype(F32)
    wide = dot(load_x_ref[...], spread, ((0,), (0,)), HIGHEST)
    wide = dot(pick, wide, precision=HIGHEST)
    wide = jnp.where(iota((512, 256), 0) % 8 == iota((512, 256), 1) % 128 // 16, wide, 0.0)
    hi, lo = split(wide)
    xb2[0:512], xb2[512:1024] = hi, lo

    for copy in loads[:NZ]:
        copy.wait()

    def pack_y(q, carry):
        lane = iota((32, 128), 1) // 4
        left = jnp.zeros((32, 128), F32)
        right = jnp.zeros((32, 128), F32)
        for p in range(32):
            s, z = q * 4 + p // 8, p % 8
            first, last = c[s, z, :, 0:128], c[s, z, :, 128:256]
            left = jnp.where(lane == p, pltpu.roll(first, 4 * p, 1) if p else first, left)
            right = jnp.where(lane == p, pltpu.roll(last, (4 * p + 4) % 128, 1) if p < 31 else last, right)
        yl[q], yr[q] = left, right
        return carry

    lax.fori_loop(0, 4, pack_y, 0)

    def pack_x(z, carry):
        low = iota((8, 256), 0) < 4
        for s in range(8):
            xn[z, s] = jnp.where(low, pltpu.roll(c[s, z, 24:32, :], 4, 0), c[s + 8, z, 24:32, :])
            xp[z, s] = jnp.where(low, c[s, z, 0:8, :], pltpu.roll(c[s + 8, z, 0:8, :], 4, 0))
        return carry

    lax.fori_loop(0, NZ, pack_x, 0)

    def presplit(z, carry):
        for s in range(NS):
            for k, (a, b) in enumerate((ROWS[1], ROWS[0])):
                both = jnp.concatenate([c[s, z, a : a + 8, :], c[s, z, b : b + 8, :]], axis=0)
                hi, lo = split(both)
                cs[s, z, 16 * k : 16 * k + 16, 0:256] = hi
                cs[s, z, 16 * k : 16 * k + 16, 256:512] = lo
        return carry

    lax.fori_loop(0, NZ, presplit, 0)
    for copy in loads[NZ:]:
        copy.wait()

    if remote:
        pl.semaphore_wait(barrier, ngy - 1 + ngx // 2 - 1 + 2)
        up_x, down_x = lax.rem(mx + 1, ngx), lax.rem(mx + ngx - 1, ngx)
        def halo(k, zg=None):
            src, dst, tx, ty = (
                (yr, hl, mx, lax.rem(my + 1, ngy)),
                (yl, hr, mx, lax.rem(my + ngy - 1, ngy)),
                (xn, hp, up_x, my),
                (xp, hn, down_x, my),
            )[k]
            slot = k
            if zg is not None:
                zs = pl.ds(2 * zg, 2)
                src, dst, slot = src.at[zs], dst.at[zs], 2 + 4 * (k - 2) + zg
            return pltpu.make_async_remote_copy(
                src, dst, halo_send.at[slot], halo_recv.at[slot], device_id={"gx": tx, "gy": ty}, device_id_type=MESH
            )

    for k in range(2):
        halo(k).start()
    for zg in range(4):
        for k in (2, 3):
            halo(k, zg).start()

    halo(0).wait_recv()
    halo(1).wait_recv()

    def unpack_y(q, carry):
        lane = iota((32, 128), 1) < 64
        left, right = hl[q], hr[q]
        pairs = (
            jnp.where(lane, right, pltpu.roll(left, 64, 1)),
            jnp.where(lane, pltpu.roll(right, 64, 1), left),
        )
        for p in range(32):
            s, z = q * 4 + p // 8, p % 8
            k = 4 * (p % 16)
            both = pairs[p // 16]
            both = pltpu.roll(both, 128 - k, 1) if k else both
            both = jnp.concatenate([both[0:8], both[24:32], both[8:24]], axis=0)
            hi, lo = split(both)
            cs[s, z, :, 512:640] = hi
            cs[s, z, :, 640:768] = lo
        return carry

    lax.fori_loop(0, 4, unpack_y, 0)

    def step(half, z):
        kept = 0 if half == 1 else 16
        sources = []
        for t in range(2):
            r0 = ROWS[half][t]
            minus = -1.0 / temp[z, r0 : r0 + 8, :]
            for k in range(NR // 2):
                if k % 8 == 0:
                    pass
                rates = []
                for r in (2 * k, 2 * k + 1):
                    product = c[r % NS, z, r0 : r0 + 8, :] * c[(3 * r + 1) % NS, z, r0 : r0 + 8, :]
                    rates.append(jnp.exp(act_ref[r] * minus) * product)
                hi, lo = split(jnp.concatenate(rates, axis=0))
                rhi[t, 16 * k : 16 * k + 16, :] = hi
                rlo[t, 16 * k : 16 * k + 16, :] = lo
            both = dot(w2[...], rhi[t])
            sources.append(both[0:128] + both[128:256] + dot(w2[0:128], rlo[t]))
        if half == 1:
            ghost = jnp.concatenate([hp[z].reshape(64, 256), hn[z].reshape(64, 256)], axis=0)
            ghost = jnp.concatenate(split(ghost), axis=0)
        for b in range(2):
            sb = slice(8 * b, 8 * b + 8)
            oy = dot(cs[sb, z, kept : kept + 16, :].reshape(128, 768), by[...])
            field = jnp.concatenate(
                [cs[sb, z, :, 0:256].reshape(256, 256), cs[sb, z, :, 256:512].reshape(256, 256)], axis=0
            )
            ox = dot(am[half], field)
            if half == 1:
                ox = ox + dot(ah[b], ghost)
            oy = oy.reshape(8, 16, 512)
            ox1, ox2 = ox[0:128].reshape(8, 16, 256), ox[128:256].reshape(8, 16, 256)
            tiles = []
            for t in range(2):
                r0 = ROWS[half][t]
                rt = slice(8 * t, 8 * t + 8)
                fx = vx[z, r0 : r0 + 8, :] * K_X
                fy = vy[z, r0 : r0 + 8, :] * K_X
                new = c[sb, z, r0 : r0 + 8, :] * CENTRE + sources[t].reshape(16, 8, 256)[sb]
                new = new + (ox2[:, rt] + oy[:, rt, 256:512]) * K_2
                new = new + fx * ox1[:, rt] + fy * oy[:, rt, 0:256]
                out_ref[sb, z, r0 : r0 + 8, :] = new
                tiles.append(new)
            hi, lo = split(jnp.concatenate(tiles, axis=1).reshape(128, 256))
            nhi[128 * b : 128 * b + 128, :] = hi
            nlo[128 * b : 128 * b + 128, :] = lo
        both = dot(vt2[...], nhi[...], ((1,), (1,)))
        total = both[0:64] + both[64:128] + dot(vt2[0:64], nlo[...], ((1,), (1,)))
        part[:, half, z] = total.reshape(8, 8, 256)

    def send_part(half, d, zs=slice(None)):
        return pltpu.make_async_remote_copy(
            part.at[gy_peer[d], half, zs],
            got.at[d - 1, half, zs],
            part_send.at[half, d - 1],
            part_recv.at[half, d - 1],
            device_id={"gx": mx, "gy": gy_peer[d]},
            device_id_type=MESH,
        )

    for half in range(2):

        def group(zg, carry, half=half):
            def one(k, inner):
                step(half, 2 * zg + k)
                return inner

            if half == 1:
                halo(2, zg).wait_recv()
                halo(3, zg).wait_recv()
            lax.fori_loop(0, 2, one, 0)
            for d in GY_ORDER:
                send_part(half, d, pl.ds(2 * zg, 2)).start()
            return carry

        lax.fori_loop(0, 4, group, 0)

    for half in range(2):
        total = part[my, half].reshape(64, 256)
        for d in GY_ORDER[::-1]:
            send_part(half, d).wait_recv()
            total = total + got[d - 1, half].reshape(64, 256)
        hi, lo = split(total)
        for h in range(2):
            yhi[64 * h : 64 * h + 64, 128 * half : 128 * half + 128] = hi[:, 128 * h : 128 * h + 128]
            ylo[64 * h : 64 * h + 64, 128 * half : 128 * half + 128] = lo[:, 128 * h : 128 * h + 128]
    both = dot(xb2[...], yhi[...], ((1,), (1,)))
    total = both[0:512] + both[512:1024] + dot(xb2[0:512], ylo[...], ((1,), (1,)))
    g[...] = total.reshape(2, 16, 2, 8, 128)

    if remote:
        pair = pltpu.make_async_remote_copy(
            g.at[1 - par],
            pair_got,
            pair_sems.at[0],
            pair_sems.at[1],
            device_id={"gx": partner, "gy": my},
            device_id_type=MESH,
        )
        pair.start()
        pair.wait_recv()
        gs[...] = g[par] + pair_got[...]
        spread_out = []
        for d in GX_ORDER:
            copy = pltpu.make_async_remote_copy(
                gs.at[chip_peer[d]],
                core_got.at[d - 1],
                core_send.at[d - 1],
                core_recv.at[d - 1],
                device_id={"gx": 2 * chip_peer[d] + par, "gy": my},
                device_id_type=MESH,
            )
            copy.start()
            spread_out.append(copy)
        total = gs[chip]
        for d, copy in list(zip(GX_ORDER, spread_out))[::-1]:
            copy.wait_recv()
            total = total + core_got[d - 1]
    else:
        total = g[0, 0]

    a, b = iota((128, 128), 0), iota((128, 128), 1)
    swap = (a == b // 64 * 64 + b % 8 * 8 + b % 64 // 8).astype(F32)
    total = dot(total.reshape(16, 128), swap, precision=HIGHEST).reshape(2, 8, 128)
    sub, lane = iota((8, 128), 0), iota((8, 128), 1) % 64 // 8
    for i in range(2):
        tile = total[i]
        result = jnp.zeros((8, 128), F32)
        for d in range(8):
            turned = pltpu.roll(tile, d, 0) if d else tile
            if d:
                turned = jnp.where(
                    lane + d < 8, pltpu.roll(turned, 128 - 8 * d, 1), pltpu.roll(turned, 64 - 8 * d, 1)
                )
            result = jnp.where(lane == (sub - d + 8) % 8, turned, result)
        core_ref[i] = result

    if remote:
        for k in range(2):
            halo(k).wait_send()
        for zg in range(4):
            for k in (2, 3):
                halo(k, zg).wait_send()
        for half in range(2):
            for d in GY_ORDER:
                send_part(half, d).wait_send()
        pair.wait_send()
        for copy in spread_out:
            copy.wait_send()


def section(c, vx, vy, temp, pref, act, stoich, load_x, load_y, remote=True, ngx=32, ngy=8):
    vmem = pl.BlockSpec(memory_space=pltpu.VMEM)
    smem = pl.BlockSpec(memory_space=pltpu.SMEM)
    hbm = pl.BlockSpec(memory_space=pltpu.HBM)
    scratch = [
        pltpu.VMEM((NS, NZ, CX, CY_), F32),
        pltpu.VMEM((NZ, CX, CY_), F32),
        pltpu.VMEM((NZ, CX, CY_), F32),
        pltpu.VMEM((NZ, CX, CY_), F32),
        pltpu.VMEM(BY.shape, BF16),
        pltpu.VMEM(AMAIN.shape, BF16),
        pltpu.VMEM(AHALO.shape, BF16),
        pltpu.VMEM((NS, NZ, CX, 768), BF16),
        pltpu.VMEM((NZ, 8, 8, CY_), F32),
        pltpu.VMEM((NZ, 8, 8, CY_), F32),
        pltpu.VMEM((NZ, 8, 8, CY_), F32),
        pltpu.VMEM((NZ, 8, 8, CY_), F32),
        pltpu.VMEM((4, CX, 128), F32),
        pltpu.VMEM((4, CX, 128), F32),
        pltpu.VMEM((4, CX, 128), F32),
        pltpu.VMEM((4, CX, 128), F32),
        pltpu.VMEM((256, 256), BF16),
        pltpu.VMEM((128, 256), BF16),
        pltpu.VMEM((1024, 256), BF16),
        pltpu.VMEM((2, 256, 256), BF16),
        pltpu.VMEM((2, 256, 256), BF16),
        pltpu.VMEM((256, 256), BF16),
        pltpu.VMEM((256, 256), BF16),
        pltpu.VMEM((8, 2, NZ, 8, 256), F32),
        pltpu.VMEM((7, 2, NZ, 8, 256), F32),
        pltpu.VMEM((128, 256), BF16),
        pltpu.VMEM((128, 256), BF16),
        pltpu.VMEM((2, 16, 2, 8, 128), F32),
        pltpu.VMEM((16, 2, 8, 128), F32),
        pltpu.VMEM((16, 2, 8, 128), F32),
        pltpu.VMEM((15, 2, 8, 128), F32),
        pltpu.SemaphoreType.DMA((NZ + 6,)),
        pltpu.SemaphoreType.DMA((10,)),
        pltpu.SemaphoreType.DMA((10,)),
        pltpu.SemaphoreType.DMA((2, 7)),
        pltpu.SemaphoreType.DMA((2, 7)),
        pltpu.SemaphoreType.DMA((2,)),
        pltpu.SemaphoreType.DMA((15,)),
        pltpu.SemaphoreType.DMA((15,)),
    ]
    params = dict(vmem_limit_bytes=59 * 1024 * 1024)
    if remote:
        params.update(collective_id=0, has_side_effects=True)
    return pl.pallas_call(
        functools.partial(kernel, remote, ngx, ngy),
        name="section",
        out_shape=(
            pltpu.VMEM((NS, NZ, CX, CY_), F32),
            pltpu.VMEM((2, 8, 128), F32),
        ),
        in_specs=[smem, vmem, vmem, vmem, vmem] + [hbm] * 7,
        out_specs=(vmem, vmem),
        scratch_shapes=scratch,
        compiler_params=pltpu.CompilerParams(**params),
    )(
        act,
        pref.reshape(1, NR),
        stoich.T,
        load_x,
        load_y.T,
        c,
        vx,
        vy,
        temp,
        jnp.asarray(BY),
        jnp.asarray(AMAIN),
        jnp.asarray(AHALO),
    )


def solution(mesh):
    in_specs = (
        P(None, None, "gx", "gy"),
        P(None, "gx", "gy"),
        P(None, "gx", "gy"),
        P(None, "gx", "gy"),
        P(),
        P(),
        P(),
        P("gx", None),
        P("gy", None),
    )
    out_specs = (P(None, None, "gx", "gy"), P("gx", "gy", None))
    body = functools.partial(section, ngx=mesh.shape["gx"], ngy=mesh.shape["gy"])
    return jax.shard_map(body, mesh=mesh, in_specs=in_specs, out_specs=out_specs, check_vma=False)
```
